32 devices in a mesh: groups: 2 (over y), ctx: 4 (over z), head: 4 (over x, core).
Axes of the slice: x: 2, y: 2, z: 4, core: 2. Of those that a mesh axis runs over, the one named last changes fastest.
Arguments:
- activations: bfloat16 [16384, 1024], P(('groups', 'ctx')), parts along dimension 0, may hold values from -40 to 40
- out_grad: bfloat16 [16384, 1024], P(('groups', 'ctx')), parts along dimension 0, may hold values from -5 to 5
- segment_ids: int32 [16384], P(('groups', 'ctx')), parts along dimension 0, may hold values from 0 to 7, never falling along the last dimension, each value on 1 to 2048 neighbouring positions
- qkv_weight: bfloat16 [1024, 3072], P(None, 'head'), may hold values from -0.25 to 0.25
- out_weight: bfloat16 [1024, 1024], P(None, 'head'), may hold values from -0.1875 to 0.1875
Outputs:
- input_grad: bfloat16 [16384, 1024], P(('groups', 'ctx'), 'head'), parts along dimension 0
- qkv_weight_grad: float32 [2048, 3072], P(('groups', 'ctx'), 'head'), parts along dimension 0
- out_weight_grad: float32 [2048, 1024], P(('groups', 'ctx'), 'head'), parts along dimension 0
The draws below stay inside these ranges and needn't reach their ends.
There are 2 independent parts, one for each index of `groups`. The reference program is written for one: setup_inputs(seed, part) draws one part's arguments, and reference() takes and returns one part's arrays. A program takes and returns all parts, laid end to end along the dimension named above; an argument that names none is the same for every part. Nothing has to cross between parts.
Inputs may be any that keep to these rules, and one draw needn't show every extreme that they name: `segment_ids`: segment numbers never fall along the sequence; each document holds 1 to 2048 tokens, one exactly 2048.
All inputs are finite; a program needn't handle non-finite values.
Results may differ from the reference program's by a relative error of at most 0.025.
The reference program's roundings to bfloat16 on the way (of `projected`, `queries`, `keys`, `head_grads`, `weights_low`, `attended`, `score_grad` and `qkv_grad`) count: a program that leaves them out, or rounds other values in their place, can miss the bound.
Values may be sent and summed in bfloat16 or wider, within the bound.
A program may use at most 128 MiB of HBM per device.

```python
import math
import jax
import jax.numpy as jnp
import numpy as np
from jax import lax

D = 1024
H = 16
HD = 64
WIN = 512
QBLK = 512
TOKENS = 8192
DOCS = 8
DOC_MOST = 2048
N_HEAD = 4


def draw_activations(key, part):
    base_key = jax.random.fold_in(key, 0)
    base = jax.random.truncated_normal(base_key, -6.0, 6.0, (TOKENS, D), jnp.float32)
    return base.astype(jnp.bfloat16)


def draw_qkv_weight(key, part):
    base_key = jax.random.fold_in(key, 0)
    limit = min(6.0, 0.25 * math.sqrt(D))
    base = jax.random.truncated_normal(base_key, -limit, limit, (D, H, 3, HD), jnp.float32) / math.sqrt(D)
    return base.reshape(D, H * 3 * HD).astype(jnp.bfloat16)


def with_spikes(array, rng, source, target, blocks, factor):
    owner, partner = [(jnp.arange(array.shape[dim]) // (array.shape[dim] // blocks)).reshape([-1 if axis == dim else 1 for axis in range(array.ndim)]) for dim in (source, target)]
    chosen = jax.random.permutation(rng, blocks)[partner]
    strong = (owner == chosen) | (owner == (partner + blocks // 2) % blocks)
    return jnp.where(strong, factor * array, array)


def block_levels(key, shape, shards, low, top_value):
    level, own = 1.0, jax.random.fold_in(key, 6)
    for axis_at, shards_of in shards:
        heights = jnp.exp(jax.random.uniform(jax.random.fold_in(own, axis_at), (shards_of,), jnp.float32, low / len(shards), top_value / len(shards)))
        level = level * jnp.repeat(heights, shape[axis_at] // shards_of).reshape([-1 if axis == axis_at else 1 for axis in range(len(shape))])
    return level


def length_profile(count, total, most, slope):
    portions = [(1 << 20) // math.isqrt(grade ** slope) + 1 for grade in range(2, count + 1)]
    rest, given = total - most - (count - 1), [1] * (count - 1)
    while rest > 0:
        movable = [i for i in range(count - 1) if given[i] < most]
        pool, left = sum([portions[i] for i in movable]), rest
        for i in movable:
            more = min(most - given[i], max(1, left * portions[i] // pool), rest)
            given[i] = given[i] + more
            rest = rest - more
    return np.array([most] + given)


def uneven_parts(own_key, count, total, bound, skew):
    if count == 2:
        one = jax.random.randint(own_key, (), max(1, total - bound), min(bound, total - 1) + 1)
        return jnp.stack([one, total - one])
    sizes = jnp.asarray(length_profile(count, total, bound, skew), jnp.int32)
    couples = (count - 1) // 2
    source_of, taker = sizes[1:1 + 2 * couples:2], sizes[2:2 + 2 * couples:2]
    room = jnp.minimum(source_of - 1, bound - taker)
    moved = jax.random.randint(jax.random.fold_in(own_key, 1), (couples,), 0, 1 << 20) % (room + 1)
    sizes = sizes.at[1:1 + 2 * couples:2].set(source_of - moved).at[2:2 + 2 * couples:2].set(taker + moved)
    return sizes[jax.random.permutation(jax.random.fold_in(own_key, 2), count)]


def noise(key, shape, scale, most, cuts=(), kind=jnp.bfloat16):
    entries = jax.random.normal(key, shape, jnp.float32) * scale
    if len(cuts) > 0:
        entries = block_levels(key, shape, cuts, -0.22, 0.18) * entries
    return jnp.clip(entries, min=-most, max=most).astype(kind)


def bell_draw_with(stream_key, dims, scale, reach, pieces, heavy, kind=jnp.bfloat16):
    drawn = scale * jax.random.normal(stream_key, dims, jnp.float32)
    if pieces:
        drawn = drawn * block_levels(stream_key, dims, pieces, -0.22, 0.18)
    return jnp.clip(with_spikes(drawn, jax.random.fold_in(stream_key, 3), *heavy), -reach, reach).astype(kind)


def setup_inputs(seed: int = 0, part: int = 0) -> dict:
    keys = jax.random.split(jax.random.key(seed), 6)
    own_keys = jax.random.split(jax.random.fold_in(keys[5], part), 6)
    activations = draw_activations(jax.random.fold_in(jax.random.fold_in(keys[5], part), 71), part)
    out_grad = bell_draw_with(own_keys[1], (TOKENS, D), 0.25, 5.0, ((0, 4),), (0, 1, 4, 2.0))
    segment_ids = jnp.searchsorted(jnp.cumsum(uneven_parts(own_keys[2], DOCS, TOKENS, DOC_MOST, 2)), jnp.arange(TOKENS), side="right").astype(jnp.int32)
    qkv_weight = draw_qkv_weight(jax.random.fold_in(keys[5], 71), part)
    out_weight = noise(keys[4], (D, H * HD), (H * HD) ** -0.5, 0.1875, ((1, 4),))
    return {"activations": activations, "out_grad": out_grad, "segment_ids": segment_ids, "qkv_weight": qkv_weight, "out_weight": out_weight}


def rope_tables(first, count, width):
    middle = width // 2
    position = (first + jnp.arange(count, dtype=jnp.int32)).astype(jnp.float32)
    exponent = jnp.arange(middle, dtype=jnp.int32).astype(jnp.float32) * (2.0 / width)
    inverse = jnp.power(jnp.float32(10000.0), -exponent)
    angles = position[:, None] * inverse[None, :]
    angles = jnp.concatenate([angles, angles], axis=1)
    return jnp.cos(angles), jnp.sin(angles)


def rotate(values, cosine_table, sine_table):
    middle = values.shape[-1] // 2
    turned = jnp.concatenate([-values[..., middle:], values[..., :middle]], axis=-1)
    return values * cosine_table[:, None, :] + turned * sine_table[:, None, :]


def unrotate(gradient, cosine_table, sine_table):
    middle = gradient.shape[-1] // 2
    scaled = gradient * sine_table[:, None, :]
    turned = jnp.concatenate([scaled[..., middle:], -scaled[..., :middle]], axis=-1)
    return gradient * cosine_table[:, None, :] + turned


def window_mask(row_position, column_position, row_segment, column_segment, seq_total):
    inside_rows = (row_position >= 0) & (row_position < seq_total)
    inside_columns = (column_position >= 0) & (column_position < seq_total)
    within = jnp.abs(row_position[:, None] - column_position[None, :]) <= WIN
    same_doc = row_segment[:, None] == column_segment[None, :]
    return within & inside_rows[:, None] & inside_columns[None, :] & same_doc


def band_tile(query_block, key_block, value_block, grad_block, allowed):
    factor = query_block.shape[-1] ** -0.5
    visible = allowed[None, :, :]
    scores = jnp.einsum("qhd,khd->hqk", query_block.astype(jnp.float32), key_block.astype(jnp.float32)) * factor
    scores = jnp.where(visible, scores, -1e30)
    highest = jnp.max(scores, axis=-1)
    summed = jnp.sum(jnp.where(visible, jnp.exp(scores - highest[..., None]), 0.0), axis=-1)
    log_total = highest + jnp.log(summed)
    weights = jnp.where(visible, jnp.exp(scores - log_total[..., None]), 0.0)
    weights_low = weights.astype(jnp.bfloat16)
    attended = jnp.einsum("hqk,khd->qhd", weights_low.astype(jnp.float32), value_block.astype(jnp.float32)).astype(jnp.bfloat16)
    row_delta = jnp.sum(grad_block.astype(jnp.float32) * attended.astype(jnp.float32), axis=-1)
    weight_grad = jnp.einsum("qhd,khd->hqk", grad_block.astype(jnp.float32), value_block.astype(jnp.float32))
    score_grad = (weights * (weight_grad - row_delta.T[:, :, None]) * factor).astype(jnp.bfloat16)
    query_grad = jnp.einsum("hqk,khd->qhd", score_grad.astype(jnp.float32), key_block.astype(jnp.float32))
    key_grad = jnp.einsum("hqk,qhd->khd", score_grad.astype(jnp.float32), query_block.astype(jnp.float32))
    value_grad = jnp.einsum("hqk,qhd->khd", weights_low.astype(jnp.float32), grad_block.astype(jnp.float32))
    return attended, query_grad, key_grad, value_grad


def reference(activations, out_grad, segment_ids, qkv_weight, out_weight):
    tokens = TOKENS
    projected = jnp.dot(activations, qkv_weight, preferred_element_type=jnp.float32).astype(jnp.bfloat16)
    projected = projected.reshape(tokens, H, 3, HD)
    cosine_table, sine_table = rope_tables(0, tokens, HD)
    queries = rotate(projected[:, :, 0].astype(jnp.float32), cosine_table, sine_table).astype(jnp.bfloat16)
    rotated_keys = rotate(projected[:, :, 1].astype(jnp.float32), cosine_table, sine_table).astype(jnp.bfloat16)
    values = projected[:, :, 2]
    head_grads = jnp.dot(out_grad, out_weight, preferred_element_type=jnp.float32).astype(jnp.bfloat16)
    head_grads = head_grads.reshape(tokens, H, HD)
    padding = ((WIN, WIN), (0, 0), (0, 0))
    wide_keys = jnp.pad(rotated_keys, padding)
    wide_values = jnp.pad(values, padding)
    wide_segments = jnp.pad(segment_ids, (WIN, WIN))
    wide_position = jnp.arange(tokens + 2 * WIN, dtype=jnp.int32) - WIN
    own_position = jnp.arange(tokens, dtype=jnp.int32)
    span = QBLK + 2 * WIN
    blocks = tokens // QBLK

    def step(carry, block_index):
        key_acc, value_acc = carry
        start = (block_index * QBLK).astype(jnp.int32)
        allowed = window_mask(lax.dynamic_slice_in_dim(own_position, start, QBLK, 0),
                              lax.dynamic_slice_in_dim(wide_position, start, span, 0),
                              lax.dynamic_slice_in_dim(segment_ids, start, QBLK, 0),
                              lax.dynamic_slice_in_dim(wide_segments, start, span, 0), tokens)
        attended, query_grad, key_grad, value_grad = band_tile(
            lax.dynamic_slice_in_dim(queries, start, QBLK, 0),
            lax.dynamic_slice_in_dim(wide_keys, start, span, 0),
            lax.dynamic_slice_in_dim(wide_values, start, span, 0),
            lax.dynamic_slice_in_dim(head_grads, start, QBLK, 0), allowed)
        key_acc = lax.dynamic_update_slice_in_dim(key_acc, lax.dynamic_slice_in_dim(key_acc, start, span, 0) + key_grad, start, 0)
        value_acc = lax.dynamic_update_slice_in_dim(value_acc, lax.dynamic_slice_in_dim(value_acc, start, span, 0) + value_grad, start, 0)
        return (key_acc, value_acc), (attended, query_grad)

    empty = jnp.zeros((tokens + 2 * WIN, H, HD), jnp.float32)
    (key_acc, value_acc), (attended_all, query_all) = lax.scan(step, (empty, empty), jnp.arange(blocks, dtype=jnp.int32))
    attended_all = attended_all.reshape(tokens, H * HD)
    query_all = query_all.reshape(tokens, H, HD)
    key_grads = key_acc[WIN:WIN + tokens]
    value_grads = value_acc[WIN:WIN + tokens]
    query_pre = unrotate(query_all, cosine_table, sine_table)
    key_pre = unrotate(key_grads, cosine_table, sine_table)
    qkv_grad = jnp.stack([query_pre, key_pre, value_grads], axis=2).reshape(tokens, H * 3 * HD).astype(jnp.bfloat16)
    qkv_weight_grad = jnp.dot(activations.T, qkv_grad, preferred_element_type=jnp.float32)
    out_weight_grad = jnp.dot(out_grad.T, attended_all, preferred_element_type=jnp.float32)
    group_width = (H // N_HEAD) * 3 * HD
    summed = jnp.zeros((tokens, D), jnp.float32)
    for group in range(N_HEAD):
        term = jnp.dot(qkv_grad[:, group * group_width:(group + 1) * group_width],
                       qkv_weight[:, group * group_width:(group + 1) * group_width].T,
                       preferred_element_type=jnp.float32)
        term = lax.optimization_barrier(term.astype(jnp.bfloat16)).astype(jnp.float32)
        summed = summed + term
    return summed.astype(jnp.bfloat16), qkv_weight_grad, out_weight_grad
```

```python
import functools

import jax
import jax.numpy as jnp
from jax import lax
from jax.experimental import pallas as pl
from jax.experimental.pallas import tpu as pltpu
from jax.sharding import PartitionSpec as P

HD = 64
HALF = HD // 2
WIN = 512
QB = 256
SPAN = QB + 2 * WIN
KB = 256
NT = (((1,), (1,)), ((), ()))
F32 = jnp.float32
BF16 = jnp.bfloat16


def permutation(heads):
    width = heads * HD
    column = lax.broadcasted_iota(jnp.int32, (3 * width, 3 * width), 1)
    row = lax.broadcasted_iota(jnp.int32, (3 * width, 3 * width), 0)
    part = column // width
    inner = column % width
    side = inner // (width // 2)
    low = inner % (width // 2)
    rope_source = (low // HALF) * (3 * HD) + part * HD + side * HALF + low % HALF
    value_source = (inner // HD) * (3 * HD) + 2 * HD + inner % HD
    return (row == jnp.where(part == 2, value_source, rope_source)).astype(BF16)


def attention_kernel(heads, q_ref, g_ref, k_ref, v_ref, qseg_ref, kseg_ref, cos_ref, sin_ref,
                     att_ref, dq_ref, dk_ref, dv_ref, kt_ref, vt_ref, bias_ref, s_ref, w_ref, ds_ref):
    step = pl.program_id(0)
    width = heads * HD
    wide = k_ref.shape[0]

    @pl.when(step == 0)
    def _():
        dk_ref[...] = jnp.zeros_like(dk_ref)
        dv_ref[...] = jnp.zeros_like(dv_ref)

        @pl.loop(0, wide // KB)
        def _(i):
            at = pl.ds(pl.multiple_of(i * KB, KB), KB)
            kt_ref[:, at] = k_ref[at, :].T
            vt_ref[:, at] = v_ref[at, :].T

    start = pl.multiple_of(step * QB, QB)
    for t in range(SPAN // KB):
        r = t * KB + lax.broadcasted_iota(jnp.int32, (KB, QB), 0)
        c = lax.broadcasted_iota(jnp.int32, (KB, QB), 1)
        ok = (r - c >= 0) & (r - c <= 2 * WIN) & (kseg_ref[pl.ds(start + t * KB, KB), :] == qseg_ref[...])
        bias_ref[t * KB:(t + 1) * KB, :] = jnp.where(ok, 0.0, -1e30)

    lane = lax.broadcasted_iota(jnp.int32, (QB, width), 1)
    rope_head = (lane % (width // 2)) // HALF
    value_head = lane // HD
    q_all = q_ref[...]
    g_all = g_ref[...]
    zero = jnp.zeros_like(q_all)
    q_heads, g_heads, att, low, high = [], [], [], [], []
    g_t = g_all.T
    cos, sin = cos_ref[...], sin_ref[...]
    for h in range(heads):
        qh = jnp.where(rope_head == h, q_all, zero)
        gh = jnp.where(value_head == h, g_all, zero)
        q_heads.append(qh)
        g_heads.append(gh)
        cols = slice(h * QB, (h + 1) * QB)
        top = jnp.full((1, QB), -1e30, F32)
        for t in range(SPAN // KB):
            rows = slice(t * KB, (t + 1) * KB)
            s = lax.dot_general(k_ref[pl.ds(start + t * KB, KB), :], qh, NT, preferred_element_type=F32)
            s = s + bias_ref[rows, :]
            s_ref[rows, :] = s
            top = jnp.maximum(top, jnp.max(s, axis=0, keepdims=True))
        total = jnp.zeros((1, QB), F32)
        for t in range(SPAN // KB):
            rows = slice(t * KB, (t + 1) * KB)
            p = jnp.exp(s_ref[rows, :] - top)
            s_ref[rows, :] = p
            total = total + jnp.sum(p, axis=0, keepdims=True)
        scale = 1.0 / total
        out = jnp.zeros((HD, QB), F32)
        for t in range(SPAN // KB):
            rows = slice(t * KB, (t + 1) * KB)
            w = s_ref[rows, :] * scale
            s_ref[rows, :] = w
            w = w.astype(BF16)
            w_ref[rows, cols] = w
            out = out + jnp.dot(vt_ref[h * HD:(h + 1) * HD, pl.ds(start + t * KB, KB)], w,
                                preferred_element_type=F32)
        out = out.astype(BF16).astype(F32)
        att.append(out)
        delta = jnp.sum(out * g_t[h * HD:(h + 1) * HD, :].astype(F32), axis=0, keepdims=True)
        dlow = jnp.zeros((HALF, QB), F32)
        dhigh = jnp.zeros((HALF, QB), F32)
        for t in range(SPAN // KB):
            rows = slice(t * KB, (t + 1) * KB)
            at = pl.ds(start + t * KB, KB)
            dp = lax.dot_general(v_ref[at, :], gh, NT, preferred_element_type=F32)
            ds = (s_ref[rows, :] * (dp - delta)).astype(BF16)
            ds_ref[rows, cols] = ds
            kth = jnp.concatenate([kt_ref[h * HALF:(h + 1) * HALF, at],
                                   kt_ref[width // 2 + h * HALF:width // 2 + (h + 1) * HALF, at]], axis=0)
            piece = jnp.dot(kth, ds, preferred_element_type=F32)
            dlow = dlow + piece[:HALF]
            dhigh = dhigh + piece[HALF:]
        factor = HD ** -0.5
        dlow, dhigh = dlow * factor, dhigh * factor
        low.append(dlow * cos + dhigh * sin)
        high.append(dhigh * cos - dlow * sin)
    att_ref[...] = jnp.concatenate(att, axis=0).T.astype(BF16)
    dq_ref[...] = jnp.concatenate(low + high, axis=0).T.astype(BF16)
    q_cat = jnp.concatenate(q_heads, axis=0)
    g_cat = jnp.concatenate(g_heads, axis=0)
    for t in range(SPAN // KB):
        rows = slice(t * KB, (t + 1) * KB)
        at = pl.ds(start + t * KB, KB)
        dk_ref[at, :] += jnp.dot(ds_ref[rows, :], q_cat, preferred_element_type=F32)
        dv_ref[at, :] += jnp.dot(w_ref[rows, :], g_cat, preferred_element_type=F32)


def attention(queries, grads, keys, values, segment_row, segment_column, cos, sin):
    tokens, width = queries.shape
    heads = width // HD
    wide = keys.shape[0]
    whole = lambda i: (0, 0)
    block = lambda i: (i, 0)
    across = lambda i: (0, i)
    return pl.pallas_call(
        functools.partial(attention_kernel, heads),
        grid=(tokens // QB,),
        in_specs=[
            pl.BlockSpec((QB, width), block),
            pl.BlockSpec((QB, width), block),
            pl.BlockSpec((wide, width), whole),
            pl.BlockSpec((wide, width), whole),
            pl.BlockSpec((1, QB), across),
            pl.BlockSpec((wide, 1), whole),
            pl.BlockSpec((HALF, QB), across),
            pl.BlockSpec((HALF, QB), across),
        ],
        out_specs=[
            pl.BlockSpec((QB, width), block),
            pl.BlockSpec((QB, width), block),
            pl.BlockSpec((wide, width), whole),
            pl.BlockSpec((wide, width), whole),
        ],
        out_shape=[
            jax.ShapeDtypeStruct((tokens, width), BF16),
            jax.ShapeDtypeStruct((tokens, width), BF16),
            jax.ShapeDtypeStruct((wide, width), F32),
            jax.ShapeDtypeStruct((wide, width), F32),
        ],
        scratch_shapes=[
            pltpu.VMEM((width, wide), BF16),
            pltpu.VMEM((width, wide), BF16),
            pltpu.VMEM((SPAN, QB), F32),
            pltpu.VMEM((SPAN, QB), F32),
            pltpu.VMEM((SPAN, heads * QB), BF16),
            pltpu.VMEM((SPAN, heads * QB), BF16),
        ],
        compiler_params=pltpu.CompilerParams(
            dimension_semantics=("arbitrary",), vmem_limit_bytes=48 * 1024 * 1024
        ),
        cost_estimate=pl.CostEstimate(
            flops=12 * tokens * SPAN * width, bytes_accessed=16 * wide * width,
            transcendentals=tokens * SPAN * heads
        ),
    )(queries, grads, keys, values, segment_row, segment_column, cos, sin)


def exchange(low_rim, high_rim):
    count = lax.axis_size("ctx")
    forward = [(i, i + 1) for i in range(count - 1)]
    backward = [(i + 1, i) for i in range(count - 1)]
    return lax.ppermute(high_rim, "ctx", forward), lax.ppermute(low_rim, "ctx", backward)


def local(activations, out_grad, segment_ids, qkv_weight, out_weight):
    tokens = activations.shape[0]
    columns = qkv_weight.shape[1]
    width = columns // 3
    heads = width // HD
    half = width // 2
    devices = lax.axis_size("ctx")
    me = lax.axis_index("ctx")
    position = (me * tokens + jnp.arange(tokens, dtype=jnp.int32)).astype(F32)
    exponent = jnp.arange(HALF, dtype=jnp.int32).astype(F32) * (2.0 / HD)
    inverse = jnp.power(F32(10000.0), -exponent)
    angles = inverse[:, None] * position[None, :]
    cos_t, sin_t = lax.optimization_barrier((jnp.cos(angles), jnp.sin(angles)))
    cos = jnp.tile(cos_t.T, (1, heads))
    sin = jnp.tile(sin_t.T, (1, heads))

    order = permutation(heads)
    weight = jnp.dot(qkv_weight, order, preferred_element_type=F32).astype(BF16)

    def rope(block):
        block = block.astype(F32)
        low, high = block[:, :half], block[:, half:]
        return jnp.concatenate([low * cos - high * sin, high * cos + low * sin], axis=1)

    key_value = jnp.dot(activations, weight[:, width:], preferred_element_type=F32).astype(BF16)
    keys = rope(key_value[:, :width]).astype(BF16)
    values = key_value[:, width:]
    pairs = jnp.concatenate([keys, values], axis=1)
    low_halo, high_halo = exchange(pairs[:WIN], pairs[tokens - WIN:])
    low_seg, high_seg = exchange(segment_ids[:WIN], segment_ids[tokens - WIN:])
    low_seg = jnp.where(me == 0, -1, low_seg)
    high_seg = jnp.where(me == devices - 1, -1, high_seg)
    wide_seg = jnp.concatenate([low_seg, segment_ids, high_seg])
    queries = jnp.dot(activations, weight[:, :width], preferred_element_type=F32).astype(BF16)
    queries = (rope(queries).astype(BF16) * BF16(HD ** -0.5)).astype(BF16)
    head_grads = jnp.dot(out_grad, out_weight, preferred_element_type=F32).astype(BF16)
    wide_keys = jnp.concatenate([low_halo[:, :width], keys, high_halo[:, :width]], axis=0)
    wide_values = jnp.concatenate([low_halo[:, width:], values, high_halo[:, width:]], axis=0)

    attended, query_grad, key_grad, value_grad = attention(
        queries, head_grads, wide_keys, wide_values, segment_ids[None, :], wide_seg[:, None], cos_t, sin_t
    )

    rim_low = jnp.concatenate([key_grad[:WIN], value_grad[:WIN]], axis=1).astype(BF16)
    rim_high = jnp.concatenate([key_grad[tokens + WIN:], value_grad[tokens + WIN:]], axis=1).astype(BF16)
    from_low, from_high = exchange(rim_low, rim_high)
    out_part = lax.dot_general(out_grad, attended, (((0,), (0,)), ((), ())), preferred_element_type=F32)
    arrived = jnp.concatenate(
        [from_low, jnp.zeros((tokens - 2 * WIN, 2 * width), BF16), from_high], axis=0
    ).astype(F32)
    key_grad = key_grad[WIN:WIN + tokens] + arrived[:, :width]
    value_grad = value_grad[WIN:WIN + tokens] + arrived[:, width:]
    low, high = key_grad[:, :half], key_grad[:, half:]
    qkv_grad = jnp.concatenate(
        [query_grad, (low * cos + high * sin).astype(BF16), (high * cos - low * sin).astype(BF16),
         value_grad.astype(BF16)], axis=1
    )
    input_term = lax.dot_general(qkv_grad, weight, NT, preferred_element_type=F32)
    input_grad = lax.psum_scatter(
        input_term.astype(BF16), "head", scatter_dimension=1, tiled=True
    )
    qkv_part = lax.dot_general(activations, qkv_grad, (((0,), (0,)), ((), ())), preferred_element_type=F32)
    qkv_part = lax.dot_general(qkv_part.astype(BF16), order, NT, preferred_element_type=F32)
    gradients = lax.psum_scatter(
        jnp.concatenate([qkv_part.astype(BF16), out_part.astype(BF16)], axis=1),
        "ctx", scatter_dimension=0, tiled=True,
    ).astype(F32)
    return (input_grad, gradients[:, :columns], gradients[:, columns:])


def solution(mesh):
    in_specs = (
        P(("groups", "ctx"), None),
        P(("groups", "ctx"), None),
        P(("groups", "ctx")),
        P(None, "head"),
        P(None, "head"),
    )
    out_specs = (
        P(("groups", "ctx"), "head"),
        P(("groups", "ctx"), "head"),
        P(("groups", "ctx"), "head"),
    )
    return jax.shard_map(local, mesh=mesh, in_specs=in_specs, out_specs=out_specs, check_vma=False)
```

```python
import functools

import jax
import jax.numpy as jnp
from jax import lax
from jax.experimental import pallas as pl
from jax.experimental.pallas import tpu as pltpu
from jax.sharding import PartitionSpec as P

HD = 64
HALF = HD // 2
WIN = 512
QB = 256
SPAN = QB + 2 * WIN
KB = 256
NT = (((1,), (1,)), ((), ()))
F32 = jnp.float32
BF16 = jnp.bfloat16


def permutation(heads):
    width = heads * HD
    column = lax.broadcasted_iota(jnp.int32, (3 * width, 3 * width), 1)
    row = lax.broadcasted_iota(jnp.int32, (3 * width, 3 * width), 0)
    part = column // width
    inner = column % width
    side = inner // (width // 2)
    low = inner % (width // 2)
    rope_source = (low // HALF) * (3 * HD) + part * HD + side * HALF + low % HALF
    value_source = (inner // HD) * (3 * HD) + 2 * HD + inner % HD
    return (row == jnp.where(part == 2, value_source, rope_source)).astype(BF16)


def attention_kernel(heads, q_ref, g_ref, k_ref, v_ref, qseg_ref, kseg_ref, cos_ref, sin_ref,
                     att_ref, dq_ref, dk_ref, dv_ref, kt_ref, vt_ref, bias_ref, s_ref, w_ref, ds_ref):
    step = pl.program_id(0)
    width = heads * HD
    wide = k_ref.shape[0]

    @pl.when(step == 0)
    def _():
        dk_ref[...] = jnp.zeros_like(dk_ref)
        dv_ref[...] = jnp.zeros_like(dv_ref)

        @pl.loop(0, wide // KB)
        def _(i):
            at = pl.ds(pl.multiple_of(i * KB, KB), KB)
            kt_ref[:, at] = k_ref[at, :].T
            vt_ref[:, at] = v_ref[at, :].T

    start = pl.multiple_of(step * QB, QB)
    for t in range(SPAN // KB):
        r = t * KB + lax.broadcasted_iota(jnp.int32, (KB, QB), 0)
        c = lax.broadcasted_iota(jnp.int32, (KB, QB), 1)
        ok = (r - c >= 0) & (r - c <= 2 * WIN) & (kseg_ref[pl.ds(start + t * KB, KB), :] == qseg_ref[...])
        bias_ref[t * KB:(t + 1) * KB, :] = jnp.where(ok, 0.0, -1e30)

    lane = lax.broadcasted_iota(jnp.int32, (QB, width), 1)
    rope_head = (lane % (width // 2)) // HALF
    value_head = lane // HD
    q_all = q_ref[...]
    g_all = g_ref[...]
    zero = jnp.zeros_like(q_all)
    q_heads, g_heads, att, low, high = [], [], [], [], []
    g_t = g_all.T
    cos, sin = cos_ref[...], sin_ref[...]
    for h in range(heads):
        qh = jnp.where(rope_head == h, q_all, zero)
        gh = jnp.where(value_head == h, g_all, zero)
        q_heads.append(qh)
        g_heads.append(gh)
        cols = slice(h * QB, (h + 1) * QB)
        top = jnp.full((1, QB), -1e30, F32)
        for t in range(SPAN // KB):
            rows = slice(t * KB, (t + 1) * KB)
            s = lax.dot_general(k_ref[pl.ds(start + t * KB, KB), :], qh, NT, preferred_element_type=F32)
            s = s + bias_ref[rows, :]
            s_ref[rows, :] = s
            top = jnp.maximum(top, jnp.max(s, axis=0, keepdims=True))
        total = jnp.zeros((1, QB), F32)
        for t in range(SPAN // KB):
            rows = slice(t * KB, (t + 1) * KB)
            p = jnp.exp(s_ref[rows, :] - top)
            s_ref[rows, :] = p
            total = total + jnp.sum(p, axis=0, keepdims=True)
        scale = 1.0 / total
        out = jnp.zeros((HD, QB), F32)
        for t in range(SPAN // KB):
            rows = slice(t * KB, (t + 1) * KB)
            w = s_ref[rows, :] * scale
            s_ref[rows, :] = w
            w = w.astype(BF16)
            w_ref[rows, cols] = w
            out = out + jnp.dot(vt_ref[h * HD:(h + 1) * HD, pl.ds(start + t * KB, KB)], w,
                                preferred_element_type=F32)
        out = out.astype(BF16).astype(F32)
        att.append(out)
        delta = jnp.sum(out * g_t[h * HD:(h + 1) * HD, :].astype(F32), axis=0, keepdims=True)
        dlow = jnp.zeros((HALF, QB), F32)
        dhigh = jnp.zeros((HALF, QB), F32)
        for t in range(SPAN // KB):
            rows = slice(t * KB, (t + 1) * KB)
            at = pl.ds(start + t * KB, KB)
            dp = lax.dot_general(v_ref[at, :], gh, NT, preferred_element_type=F32)
            ds = (s_ref[rows, :] * (dp - delta)).astype(BF16)
            ds_ref[rows, cols] = ds
            kth = jnp.concatenate([kt_ref[h * HALF:(h + 1) * HALF, at],
                                   kt_ref[width // 2 + h * HALF:width // 2 + (h + 1) * HALF, at]], axis=0)
            piece = jnp.dot(kth, ds, preferred_element_type=F32)
            dlow = dlow + piece[:HALF]
            dhigh = dhigh + piece[HALF:]
        factor = HD ** -0.5
        dlow, dhigh = dlow * factor, dhigh * factor
        low.append(dlow * cos + dhigh * sin)
        high.append(dhigh * cos - dlow * sin)
    att_ref[...] = jnp.concatenate(att, axis=0).T.astype(BF16)
    dq_ref[...] = jnp.concatenate(low + high, axis=0).T.astype(BF16)
    q_cat = jnp.concatenate(q_heads, axis=0)
    g_cat = jnp.concatenate(g_heads, axis=0)
    for t in range(SPAN // KB):
        rows = slice(t * KB, (t + 1) * KB)
        at = pl.ds(start + t * KB, KB)
        dk_ref[at, :] += jnp.dot(ds_ref[rows, :], q_cat, preferred_element_type=F32)
        dv_ref[at, :] += jnp.dot(w_ref[rows, :], g_cat, preferred_element_type=F32)


def attention(queries, grads, keys, values, segment_row, segment_column, cos, sin):
    tokens, width = queries.shape
    heads = width // HD
    wide = keys.shape[0]
    whole = lambda i: (0, 0)
    block = lambda i: (i, 0)
    across = lambda i: (0, i)
    return pl.pallas_call(
        functools.partial(attention_kernel, heads),
        grid=(tokens // QB,),
        in_specs=[
            pl.BlockSpec((QB, width), block),
            pl.BlockSpec((QB, width), block),
            pl.BlockSpec((wide, width), whole),
            pl.BlockSpec((wide, width), whole),
            pl.BlockSpec((1, QB), across),
            pl.BlockSpec((wide, 1), whole),
            pl.BlockSpec((HALF, QB), across),
            pl.BlockSpec((HALF, QB), across),
        ],
        out_specs=[
            pl.BlockSpec((QB, width), block),
            pl.BlockSpec((QB, width), block),
            pl.BlockSpec((wide, width), whole),
            pl.BlockSpec((wide, width), whole),
        ],
        out_shape=[
            jax.ShapeDtypeStruct((tokens, width), BF16),
            jax.ShapeDtypeStruct((tokens, width), BF16),
            jax.ShapeDtypeStruct((wide, width), F32),
            jax.ShapeDtypeStruct((wide, width), F32),
        ],
        scratch_shapes=[
            pltpu.VMEM((width, wide), BF16),
            pltpu.VMEM((width, wide), BF16),
            pltpu.VMEM((SPAN, QB), F32),
            pltpu.VMEM((SPAN, QB), F32),
            pltpu.VMEM((SPAN, heads * QB), BF16),
            pltpu.VMEM((SPAN, heads * QB), BF16),
        ],
        compiler_params=pltpu.CompilerParams(
            dimension_semantics=("arbitrary",), vmem_limit_bytes=48 * 1024 * 1024
        ),
        cost_estimate=pl.CostEstimate(
            flops=12 * tokens * SPAN * width, bytes_accessed=16 * wide * width,
            transcendentals=tokens * SPAN * heads
        ),
    )(queries, grads, keys, values, segment_row, segment_column, cos, sin)


def exchange(low_rim, high_rim):
    count = lax.axis_size("ctx")
    forward = [(i, i + 1) for i in range(count - 1)]
    backward = [(i + 1, i) for i in range(count - 1)]
    return lax.ppermute(high_rim, "ctx", forward), lax.ppermute(low_rim, "ctx", backward)


CHUNK = 512
MESH = pl.DeviceIdType.MESH


def reduce_kernel(nx, nz, columns, g_ref, w_ref, sums_ref, in_ref, qkv_ref, out_ref,
                  send1, recv1, send2, recv2, acc, send_r, recv_r, send_l, recv_l,
                  ss1, rs1, ss2, rs2, ssr, rsr, ssl, rsl):
    head = lax.axis_index("head")
    z = lax.axis_index("ctx")
    x, core = head // 2, head % 2
    sibling = x * 2 + (1 - core)
    cols = w_ref.shape[0] // (2 * nx)
    chunks = g_ref.shape[0] // CHUNK
    rows = sums_ref.shape[0] // nz

    barrier = pltpu.get_barrier_semaphore()
    pl.semaphore_signal(barrier, inc=1, device_id={"head": sibling}, device_id_type=MESH)
    for k in range(1, nx):
        peer = ((x + k) % nx) * 2 + core
        pl.semaphore_signal(barrier, inc=1, device_id={"head": peer}, device_id_type=MESH)
    for k in range(1, nz):
        pl.semaphore_signal(barrier, inc=1, device_id={"ctx": (z + k) % nz}, device_id_type=MESH)
    pl.semaphore_wait(barrier, nx + nz - 1)

    def right(d):
        return pltpu.make_async_remote_copy(
            src_ref=send_r.at[d], dst_ref=recv_r.at[d], send_sem=ssr.at[d], recv_sem=rsr.at[d],
            device_id={"ctx": jnp.minimum(z + 1, nz - 1)}, device_id_type=MESH)

    def left(d):
        return pltpu.make_async_remote_copy(
            src_ref=send_l.at[d], dst_ref=recv_l.at[d], send_sem=ssl.at[d], recv_sem=rsl.at[d],
            device_id={"ctx": jnp.maximum(z - 1, 0)}, device_id_type=MESH)

    @pl.when(z == 0)
    def _():
        for d in range(nz - 1, 0, -1):
            send_r[d] = sums_ref[d * rows:(d + 1) * rows, :]
            right(d).start()

    @pl.when(z == nz - 1)
    def _():
        for d in range(nz - 1):
            send_l[d] = sums_ref[d * rows:(d + 1) * rows, :]
            left(d).start()

    def term(block, r):
        at = pl.ds(pl.multiple_of(block * cols, cols), cols)
        product = lax.dot_general(g_ref[r * CHUNK:(r + 1) * CHUNK, :], w_ref[at, :], NT,
                                  preferred_element_type=F32)
        return product.astype(BF16)

    def swap(k, r):
        part = slice(r * CHUNK, (r + 1) * CHUNK)
        return pltpu.make_async_remote_copy(
            src_ref=send1.at[k, part], dst_ref=recv1.at[k, part], send_sem=ss1.at[k, r],
            recv_sem=rs1.at[k, r], device_id={"head": sibling}, device_id_type=MESH)

    def cross(k, r):
        part = slice(r * CHUNK, (r + 1) * CHUNK)
        return pltpu.make_async_remote_copy(
            src_ref=send2.at[k, part], dst_ref=recv2.at[k, part], send_sem=ss2.at[k, r],
            recv_sem=rs2.at[k, r], device_id={"head": ((x + k) % nx) * 2 + core}, device_id_type=MESH)

    hops = list(range(1, nx)) + [0]
    for k in hops:
        for r in range(chunks):
            send1[k, r * CHUNK:(r + 1) * CHUNK, :] = term(((x + k) % nx) * 2 + (1 - core), r)
            swap(k, r).start()
    for k in hops:
        for r in range(chunks):
            part = slice(r * CHUNK, (r + 1) * CHUNK)
            own = term(((x + k) % nx) * 2 + core, r).astype(F32)
            swap(k, r).wait_recv()
            both = own + recv1[k, part, :].astype(F32)
            if k == 0:
                acc[part, :] = both
            else:
                send2[k, part, :] = both.astype(BF16)
                cross(k, r).start()

    for n in range(nz - 1):
        up, down = nz - 1 - n, n

        @pl.when((z > 0) & (z < up))
        def _():
            right(up).wait_recv()
            send_r[up] = (recv_r[up].astype(F32)
                          + sums_ref[up * rows:(up + 1) * rows, :].astype(F32)).astype(BF16)
            right(up).start()

        @pl.when((z < nz - 1) & (z > down))
        def _():
            left(down).wait_recv()
            send_l[down] = (recv_l[down].astype(F32)
                            + sums_ref[down * rows:(down + 1) * rows, :].astype(F32)).astype(BF16)
            left(down).start()

    for r in range(chunks):
        part = slice(r * CHUNK, (r + 1) * CHUNK)
        value = acc[part, :]
        for k in range(1, nx):
            cross(k, r).wait_recv()
            value = value + recv2[k, part, :].astype(F32)
        in_ref[part, :] = value.astype(BF16)

    for d in range(nz):
        @pl.when(z == d)
        def _():
            value = sums_ref[d * rows:(d + 1) * rows, :].astype(F32)
            if d > 0:
                right(d).wait_recv()
                value = value + recv_r[d].astype(F32)
            if d < nz - 1:
                left(d).wait_recv()
                value = value + recv_l[d].astype(F32)
            qkv_ref[...] = value[:, :columns]
            out_ref[...] = value[:, columns:]

    for k in hops:
        for r in range(chunks):
            swap(k, r).wait_send()
            if k > 0:
                cross(k, r).wait_send()
    for d in range(nz):
        if d > 0:
            @pl.when(z < d)
            def _():
                right(d).wait_send()
        if d < nz - 1:
            @pl.when(z > d)
            def _():
                left(d).wait_send()


def reduce_all(qkv_grad, weight, sums):
    tokens, columns = qkv_grad.shape
    model = weight.shape[0]
    nz = lax.axis_size("ctx")
    devices = lax.axis_size("head")
    nx = devices // 2
    cols = model // devices
    rows, wide = model // nz, sums.shape[1]
    chunks = tokens // CHUNK
    vmem = pl.BlockSpec(memory_space=pltpu.VMEM)
    dma = pltpu.SemaphoreType.DMA
    return pl.pallas_call(
        functools.partial(reduce_kernel, nx, nz, columns),
        in_specs=[vmem] * 3,
        out_specs=[vmem] * 3,
        out_shape=[
            jax.ShapeDtypeStruct((tokens, cols), BF16),
            jax.ShapeDtypeStruct((rows, columns), F32),
            jax.ShapeDtypeStruct((rows, wide - columns), F32),
        ],
        scratch_shapes=[pltpu.VMEM((nx, tokens, cols), BF16)] * 4
        + [pltpu.VMEM((tokens, cols), F32)]
        + [pltpu.VMEM((nz, rows, wide), BF16)] * 4
        + [dma((nx, chunks))] * 4
        + [dma((nz,))] * 4,
        compiler_params=pltpu.CompilerParams(
            collective_id=0, has_side_effects=True, vmem_limit_bytes=48 * 1024 * 1024
        ),
    )(qkv_grad, weight, sums)


def local(activations, out_grad, segment_ids, qkv_weight, out_weight):
    tokens = activations.shape[0]
    columns = qkv_weight.shape[1]
    width = columns // 3
    heads = width // HD
    half = width // 2
    devices = lax.axis_size("ctx")
    me = lax.axis_index("ctx")
    position = (me * tokens + jnp.arange(tokens, dtype=jnp.int32)).astype(F32)
    exponent = jnp.arange(HALF, dtype=jnp.int32).astype(F32) * (2.0 / HD)
    inverse = jnp.power(F32(10000.0), -exponent)
    angles = inverse[:, None] * position[None, :]
    cos_t, sin_t = lax.optimization_barrier((jnp.cos(angles), jnp.sin(angles)))
    cos = jnp.tile(cos_t.T, (1, heads))
    sin = jnp.tile(sin_t.T, (1, heads))

    order = permutation(heads)
    weight = jnp.dot(qkv_weight, order, preferred_element_type=F32).astype(BF16)

    def rope(block):
        block = block.astype(F32)
        low, high = block[:, :half], block[:, half:]
        return jnp.concatenate([low * cos - high * sin, high * cos + low * sin], axis=1)

    key_value = jnp.dot(activations, weight[:, width:], preferred_element_type=F32).astype(BF16)
    keys = rope(key_value[:, :width]).astype(BF16)
    values = key_value[:, width:]
    pairs = jnp.concatenate([keys, values], axis=1)
    low_halo, high_halo = exchange(pairs[:WIN], pairs[tokens - WIN:])
    low_seg, high_seg = exchange(segment_ids[:WIN], segment_ids[tokens - WIN:])
    low_seg = jnp.where(me == 0, -1, low_seg)
    high_seg = jnp.where(me == devices - 1, -1, high_seg)
    wide_seg = jnp.concatenate([low_seg, segment_ids, high_seg])
    queries = jnp.dot(activations, weight[:, :width], preferred_element_type=F32).astype(BF16)
    queries = (rope(queries).astype(BF16) * BF16(HD ** -0.5)).astype(BF16)
    head_grads = jnp.dot(out_grad, out_weight, preferred_element_type=F32).astype(BF16)
    wide_keys = jnp.concatenate([low_halo[:, :width], keys, high_halo[:, :width]], axis=0)
    wide_values = jnp.concatenate([low_halo[:, width:], values, high_halo[:, width:]], axis=0)

    attended, query_grad, key_grad, value_grad = attention(
        queries, head_grads, wide_keys, wide_values, segment_ids[None, :], wide_seg[:, None], cos_t, sin_t
    )

    rim_low = jnp.concatenate([key_grad[:WIN], value_grad[:WIN]], axis=1).astype(BF16)
    rim_high = jnp.concatenate([key_grad[tokens + WIN:], value_grad[tokens + WIN:]], axis=1).astype(BF16)
    from_low, from_high = exchange(rim_low, rim_high)
    out_part = lax.dot_general(out_grad, attended, (((0,), (0,)), ((), ())), preferred_element_type=F32)
    arrived = jnp.concatenate(
        [from_low, jnp.zeros((tokens - 2 * WIN, 2 * width), BF16), from_high], axis=0
    ).astype(F32)
    key_grad = key_grad[WIN:WIN + tokens] + arrived[:, :width]
    value_grad = value_grad[WIN:WIN + tokens] + arrived[:, width:]
    low, high = key_grad[:, :half], key_grad[:, half:]
    qkv_grad = jnp.concatenate(
        [query_grad, (low * cos + high * sin).astype(BF16), (high * cos - low * sin).astype(BF16),
         value_grad.astype(BF16)], axis=1
    )
    qkv_part = lax.dot_general(activations, qkv_grad, (((0,), (0,)), ((), ())), preferred_element_type=F32)
    qkv_part = lax.dot_general(qkv_part.astype(BF16), order, NT, preferred_element_type=F32)
    sums = jnp.concatenate([qkv_part.astype(BF16), out_part.astype(BF16)], axis=1)
    return reduce_all(qkv_grad, weight, sums)


def solution(mesh):
    in_specs = (
        P(("groups", "ctx"), None),
        P(("groups", "ctx"), None),
        P(("groups", "ctx")),
        P(None, "head"),
        P(None, "head"),
    )
    out_specs = (
        P(("groups", "ctx"), "head"),
        P(("groups", "ctx"), "head"),
        P(("groups", "ctx"), "head"),
    )
    return jax.shard_map(local, mesh=mesh, in_specs=in_specs, out_specs=out_specs, check_vma=False)
```

```python
import functools

import jax
import jax.numpy as jnp
from jax import lax
from jax.experimental import pallas as pl
from jax.experimental.pallas import tpu as pltpu
from jax.sharding import PartitionSpec as P

HD = 64
HALF = HD // 2
WIN = 512
QB = 256
SPAN = QB + 2 * WIN
KB = 256
NT = (((1,), (1,)), ((), ()))
F32 = jnp.float32
BF16 = jnp.bfloat16


def permutation(heads):
    width = heads * HD
    column = lax.broadcasted_iota(jnp.int32, (3 * width, 3 * width), 1)
    row = lax.broadcasted_iota(jnp.int32, (3 * width, 3 * width), 0)
    part = column // width
    inner = column % width
    side = inner // (width // 2)
    low = inner % (width // 2)
    rope_source = (low // HALF) * (3 * HD) + part * HD + side * HALF + low % HALF
    value_source = (inner // HD) * (3 * HD) + 2 * HD + inner % HD
    return (row == jnp.where(part == 2, value_source, rope_source)).astype(BF16)


def attention_kernel(heads, q_ref, g_ref, low_ref, own_ref, high_ref, qseg_ref, kseg_ref, cos_ref, sin_ref,
                     att_ref, dq_ref, dk_ref, dv_ref, rim_low_ref, rim_high_ref,
                     k_ref, v_ref, kt_ref, vt_ref, bias_ref, s_ref, w_ref, ds_ref):
    step = pl.program_id(0)
    width = heads * HD
    wide = k_ref.shape[0]

    @pl.when(step == 0)
    def _():
        dk_ref[...] = jnp.zeros_like(dk_ref)
        dv_ref[...] = jnp.zeros_like(dv_ref)

        base = 0
        for source in (low_ref, own_ref, high_ref):
            @pl.loop(0, source.shape[0] // KB)
            def _(i):
                pair = source[pl.ds(pl.multiple_of(i * KB, KB), KB), :]
                at = pl.ds(pl.multiple_of(base + i * KB, KB), KB)
                k_ref[at, :] = pair[:, :width]
                v_ref[at, :] = pair[:, width:]
                kt_ref[:, at] = pair[:, :width].T
                vt_ref[:, at] = pair[:, width:].T

            base += source.shape[0]

    start = pl.multiple_of(step * QB, QB)
    for t in range(SPAN // KB):
        r = t * KB + lax.broadcasted_iota(jnp.int32, (KB, QB), 0)
        c = lax.broadcasted_iota(jnp.int32, (KB, QB), 1)
        ok = (r - c >= 0) & (r - c <= 2 * WIN) & (kseg_ref[pl.ds(start + t * KB, KB), :] == qseg_ref[...])
        bias_ref[t * KB:(t + 1) * KB, :] = jnp.where(ok, 0.0, -1e30)

    lane = lax.broadcasted_iota(jnp.int32, (QB, width), 1)
    rope_head = (lane % (width // 2)) // HALF
    value_head = lane // HD
    q_all = q_ref[...]
    g_all = g_ref[...]
    zero = jnp.zeros_like(q_all)
    q_heads, g_heads, att, low, high = [], [], [], [], []
    g_t = g_all.T
    cos, sin = cos_ref[...], sin_ref[...]

    def score(h):
        qh = jnp.where(rope_head == h, q_all, zero)
        gh = jnp.where(value_head == h, g_all, zero)
        q_heads.append(qh)
        g_heads.append(gh)
        cols = slice(h * QB, (h + 1) * QB)
        top = jnp.full((1, QB), -1e30, F32)
        for t in range(SPAN // KB):
            rows = slice(t * KB, (t + 1) * KB)
            s = lax.dot_general(k_ref[pl.ds(start + t * KB, KB), :], qh, NT, preferred_element_type=F32)
            s = s + bias_ref[rows, :]
            s_ref[rows, cols] = s
            top = jnp.maximum(top, jnp.max(s, axis=0, keepdims=True))
        return top

    top_next = score(0)
    for h in range(heads):
        top = top_next
        if h + 1 < heads:
            top_next = score(h + 1)
        gh = g_heads[h]
        cols = slice(h * QB, (h + 1) * QB)
        total = jnp.zeros((1, QB), F32)
        for t in range(SPAN // KB):
            rows = slice(t * KB, (t + 1) * KB)
            p = jnp.exp(s_ref[rows, cols] - top)
            s_ref[rows, cols] = p
            total = total + jnp.sum(p, axis=0, keepdims=True)
        scale = 1.0 / total
        out = jnp.zeros((HD, QB), F32)
        for t in range(SPAN // KB):
            rows = slice(t * KB, (t + 1) * KB)
            w = s_ref[rows, cols] * scale
            s_ref[rows, cols] = w
            w = w.astype(BF16)
            w_ref[rows, cols] = w
            out = out + jnp.dot(vt_ref[h * HD:(h + 1) * HD, pl.ds(start + t * KB, KB)], w,
                                preferred_element_type=F32)
        out = out.astype(BF16).astype(F32)
        att.append(out)
        delta = jnp.sum(out * g_t[h * HD:(h + 1) * HD, :].astype(F32), axis=0, keepdims=True)
        dlow = jnp.zeros((HALF, QB), F32)
        dhigh = jnp.zeros((HALF, QB), F32)
        for t in range(SPAN // KB):
            rows = slice(t * KB, (t + 1) * KB)
            at = pl.ds(start + t * KB, KB)
            dp = lax.dot_general(v_ref[at, :], gh, NT, preferred_element_type=F32)
            ds = (s_ref[rows, cols] * (dp - delta)).astype(BF16)
            ds_ref[rows, cols] = ds
            kth = jnp.concatenate([kt_ref[h * HALF:(h + 1) * HALF, at],
                                   kt_ref[width // 2 + h * HALF:width // 2 + (h + 1) * HALF, at]], axis=0)
            piece = jnp.dot(kth, ds, preferred_element_type=F32)
            dlow = dlow + piece[:HALF]
            dhigh = dhigh + piece[HALF:]
        factor = HD ** -0.5
        dlow, dhigh = dlow * factor, dhigh * factor
        low.append(dlow * cos + dhigh * sin)
        high.append(dhigh * cos - dlow * sin)
    att_ref[...] = jnp.concatenate(att, axis=0).T.astype(BF16)
    dq_ref[...] = jnp.concatenate(low + high, axis=0).T.astype(BF16)
    q_cat = jnp.concatenate(q_heads, axis=0)
    g_cat = jnp.concatenate(g_heads, axis=0)
    for t in range(SPAN // KB):
        rows = slice(t * KB, (t + 1) * KB)
        at = pl.ds(start + t * KB, KB)
        dk_ref[at, :] += jnp.dot(ds_ref[rows, :], q_cat, preferred_element_type=F32)
        dv_ref[at, :] += jnp.dot(w_ref[rows, :], g_cat, preferred_element_type=F32)

    @pl.when(step == pl.num_programs(0) - 1)
    def _():
        rim_low_ref[:, :width] = dk_ref[:WIN, :].astype(BF16)
        rim_low_ref[:, width:] = dv_ref[:WIN, :].astype(BF16)
        rim_high_ref[:, :width] = dk_ref[wide - WIN:, :].astype(BF16)
        rim_high_ref[:, width:] = dv_ref[wide - WIN:, :].astype(BF16)


def attention(queries, grads, low, pairs, high, segment_row, segment_column, cos, sin):
    tokens, width = queries.shape
    heads = width // HD
    wide = tokens + 2 * WIN
    whole = lambda i: (0, 0)
    block = lambda i: (i, 0)
    across = lambda i: (0, i)
    return pl.pallas_call(
        functools.partial(attention_kernel, heads),
        grid=(tokens // QB,),
        in_specs=[
            pl.BlockSpec((QB, width), block),
            pl.BlockSpec((QB, width), block),
            pl.BlockSpec((WIN, 2 * width), whole),
            pl.BlockSpec((tokens, 2 * width), whole),
            pl.BlockSpec((WIN, 2 * width), whole),
            pl.BlockSpec((1, QB), across),
            pl.BlockSpec((wide, 1), whole),
            pl.BlockSpec((HALF, QB), across),
            pl.BlockSpec((HALF, QB), across),
        ],
        out_specs=[
            pl.BlockSpec((QB, width), block),
            pl.BlockSpec((QB, width), block),
            pl.BlockSpec((wide, width), whole),
            pl.BlockSpec((wide, width), whole),
            pl.BlockSpec((WIN, 2 * width), whole),
            pl.BlockSpec((WIN, 2 * width), whole),
        ],
        out_shape=[
            jax.ShapeDtypeStruct((tokens, width), BF16),
            jax.ShapeDtypeStruct((tokens, width), BF16),
            jax.ShapeDtypeStruct((wide, width), F32),
            jax.ShapeDtypeStruct((wide, width), F32),
            jax.ShapeDtypeStruct((WIN, 2 * width), BF16),
            jax.ShapeDtypeStruct((WIN, 2 * width), BF16),
        ],
        scratch_shapes=[
            pltpu.VMEM((wide, width), BF16),
            pltpu.VMEM((wide, width), BF16),
            pltpu.VMEM((width, wide), BF16),
            pltpu.VMEM((width, wide), BF16),
            pltpu.VMEM((SPAN, QB), F32),
            pltpu.VMEM((SPAN, heads * QB), F32),
            pltpu.VMEM((SPAN, heads * QB), BF16),
            pltpu.VMEM((SPAN, heads * QB), BF16),
        ],
        compiler_params=pltpu.CompilerParams(
            dimension_semantics=("arbitrary",), vmem_limit_bytes=48 * 1024 * 1024
        ),
        cost_estimate=pl.CostEstimate(
            flops=12 * tokens * SPAN * width, bytes_accessed=16 * wide * width,
            transcendentals=tokens * SPAN * heads
        ),
    )(queries, grads, low, pairs, high, segment_row, segment_column, cos, sin)


def exchange(low_rim, high_rim):
    count = lax.axis_size("ctx")
    forward = [(i, i + 1) for i in range(count - 1)]
    backward = [(i + 1, i) for i in range(count - 1)]
    return lax.ppermute(high_rim, "ctx", forward), lax.ppermute(low_rim, "ctx", backward)


CHUNK = 512
MESH = pl.DeviceIdType.MESH


def reduce_kernel(nx, nz, columns, g_ref, w_ref, sums_ref, in_ref, qkv_ref, out_ref,
                  send1, recv1, send2, recv2, acc, send_r, recv_r, send_l, recv_l,
                  ss1, rs1, ss2, rs2, ssr, rsr, ssl, rsl):
    head = lax.axis_index("head")
    z = lax.axis_index("ctx")
    x, core = head // 2, head % 2
    sibling = x * 2 + (1 - core)
    cols = w_ref.shape[0] // (2 * nx)
    chunks = g_ref.shape[0] // CHUNK
    rows = sums_ref.shape[0] // nz

    barrier = pltpu.get_barrier_semaphore()
    pl.semaphore_signal(barrier, inc=1, device_id={"head": sibling}, device_id_type=MESH)
    for k in range(1, nx):
        peer = ((x + k) % nx) * 2 + core
        pl.semaphore_signal(barrier, inc=1, device_id={"head": peer}, device_id_type=MESH)
    for k in range(1, nz):
        pl.semaphore_signal(barrier, inc=1, device_id={"ctx": (z + k) % nz}, device_id_type=MESH)
    pl.semaphore_wait(barrier, nx + nz - 1)

    def right(d):
        return pltpu.make_async_remote_copy(
            src_ref=send_r.at[d], dst_ref=recv_r.at[d], send_sem=ssr.at[d], recv_sem=rsr.at[d],
            device_id={"ctx": jnp.minimum(z + 1, nz - 1)}, device_id_type=MESH)

    def left(d):
        return pltpu.make_async_remote_copy(
            src_ref=send_l.at[d], dst_ref=recv_l.at[d], send_sem=ssl.at[d], recv_sem=rsl.at[d],
            device_id={"ctx": jnp.maximum(z - 1, 0)}, device_id_type=MESH)

    @pl.when(z == 0)
    def _():
        for d in range(nz - 1, 0, -1):
            send_r[d] = sums_ref[d * rows:(d + 1) * rows, :]
            right(d).start()

    @pl.when(z == nz - 1)
    def _():
        for d in range(nz - 1):
            send_l[d] = sums_ref[d * rows:(d + 1) * rows, :]
            left(d).start()

    def term(block, r):
        at = pl.ds(pl.multiple_of(block * cols, cols), cols)
        product = lax.dot_general(g_ref[r * CHUNK:(r + 1) * CHUNK, :], w_ref[at, :], NT,
                                  preferred_element_type=F32)
        return product.astype(BF16)

    def swap(k, r):
        part = slice(r * CHUNK, (r + 1) * CHUNK)
        return pltpu.make_async_remote_copy(
            src_ref=send1.at[k, part], dst_ref=recv1.at[k, part], send_sem=ss1.at[k, r],
            recv_sem=rs1.at[k, r], device_id={"head": sibling}, device_id_type=MESH)

    def cross(k, r):
        part = slice(r * CHUNK, (r + 1) * CHUNK)
        return pltpu.make_async_remote_copy(
            src_ref=send2.at[k, part], dst_ref=recv2.at[k, part], send_sem=ss2.at[k, r],
            recv_sem=rs2.at[k, r], device_id={"head": ((x + k) % nx) * 2 + core}, device_id_type=MESH)

    hops = list(range(1, nx)) + [0]
    for k in hops:
        for r in range(chunks):
            send1[k, r * CHUNK:(r + 1) * CHUNK, :] = term(((x + k) % nx) * 2 + (1 - core), r)
            swap(k, r).start()
    for k in hops:
        for r in range(chunks):
            part = slice(r * CHUNK, (r + 1) * CHUNK)
            own = term(((x + k) % nx) * 2 + core, r).astype(F32)
            swap(k, r).wait_recv()
            both = own + recv1[k, part, :].astype(F32)
            if k == 0:
                acc[part, :] = both
            else:
                send2[k, part, :] = both.astype(BF16)
                cross(k, r).start()

    for n in range(nz - 1):
        up, down = nz - 1 - n, n

        @pl.when((z > 0) & (z < up))
        def _():
            right(up).wait_recv()
            send_r[up] = (recv_r[up].astype(F32)
                          + sums_ref[up * rows:(up + 1) * rows, :].astype(F32)).astype(BF16)
            right(up).start()

        @pl.when((z < nz - 1) & (z > down))
        def _():
            left(down).wait_recv()
            send_l[down] = (recv_l[down].astype(F32)
                            + sums_ref[down * rows:(down + 1) * rows, :].astype(F32)).astype(BF16)
            left(down).start()

    for r in range(chunks):
        part = slice(r * CHUNK, (r + 1) * CHUNK)
        value = acc[part, :]
        for k in range(1, nx):
            cross(k, r).wait_recv()
            value = value + recv2[k, part, :].astype(F32)
        in_ref[part, :] = value.astype(BF16)

    for d in range(nz):
        @pl.when(z == d)
        def _():
            value = sums_ref[d * rows:(d + 1) * rows, :].astype(F32)
            if d > 0:
                right(d).wait_recv()
                value = value + recv_r[d].astype(F32)
            if d < nz - 1:
                left(d).wait_recv()
                value = value + recv_l[d].astype(F32)
            qkv_ref[...] = value[:, :columns]
            out_ref[...] = value[:, columns:]

    for k in hops:
        for r in range(chunks):
            swap(k, r).wait_send()
            if k > 0:
                cross(k, r).wait_send()
    for d in range(nz):
        if d > 0:
            @pl.when(z < d)
            def _():
                right(d).wait_send()
        if d < nz - 1:
            @pl.when(z > d)
            def _():
                left(d).wait_send()


def reduce_all(qkv_grad, weight, sums):
    tokens, columns = qkv_grad.shape
    model = weight.shape[0]
    nz = lax.axis_size("ctx")
    devices = lax.axis_size("head")
    nx = devices // 2
    cols = model // devices
    rows, wide = model // nz, sums.shape[1]
    chunks = tokens // CHUNK
    vmem = pl.BlockSpec(memory_space=pltpu.VMEM)
    dma = pltpu.SemaphoreType.DMA
    return pl.pallas_call(
        functools.partial(reduce_kernel, nx, nz, columns),
        in_specs=[vmem] * 3,
        out_specs=[vmem] * 3,
        out_shape=[
            jax.ShapeDtypeStruct((tokens, cols), BF16),
            jax.ShapeDtypeStruct((rows, columns), F32),
            jax.ShapeDtypeStruct((rows, wide - columns), F32),
        ],
        scratch_shapes=[pltpu.VMEM((nx, tokens, cols), BF16)] * 4
        + [pltpu.VMEM((tokens, cols), F32)]
        + [pltpu.VMEM((nz, rows, wide), BF16)] * 4
        + [dma((nx, chunks))] * 4
        + [dma((nz,))] * 4,
        compiler_params=pltpu.CompilerParams(
            collective_id=0, has_side_effects=True, vmem_limit_bytes=48 * 1024 * 1024
        ),
    )(qkv_grad, weight, sums)


def local(activations, out_grad, segment_ids, qkv_weight, out_weight):
    tokens = activations.shape[0]
    columns = qkv_weight.shape[1]
    width = columns // 3
    heads = width // HD
    half = width // 2
    devices = lax.axis_size("ctx")
    me = lax.axis_index("ctx")
    position = (me * tokens + jnp.arange(tokens, dtype=jnp.int32)).astype(F32)
    exponent = jnp.arange(HALF, dtype=jnp.int32).astype(F32) * (2.0 / HD)
    inverse = jnp.power(F32(10000.0), -exponent)
    angles = inverse[:, None] * position[None, :]
    cos_t, sin_t = lax.optimization_barrier((jnp.cos(angles), jnp.sin(angles)))
    spread = (lax.broadcasted_iota(jnp.int32, (2 * HALF, 2 * half), 0)
              == (lambda c: (c // half) * HALF + c % HALF)(
                  lax.broadcasted_iota(jnp.int32, (2 * HALF, 2 * half), 1))).astype(F32)
    tables = lax.dot_general(jnp.concatenate([cos_t, sin_t], axis=0), spread, (((0,), (0,)), ((), ())),
                             precision=lax.Precision.HIGHEST, preferred_element_type=F32)
    cos, sin = tables[:, :half], tables[:, half:]

    order = permutation(heads)
    weight = jnp.dot(qkv_weight, order, preferred_element_type=F32).astype(BF16)

    def rope(block):
        block = block.astype(F32)
        low, high = block[:, :half], block[:, half:]
        return jnp.concatenate([low * cos - high * sin, high * cos + low * sin], axis=1)

    key_value = jnp.dot(activations, weight[:, width:], preferred_element_type=F32).astype(BF16)
    keys = rope(key_value[:, :width]).astype(BF16)
    values = key_value[:, width:]
    pairs = jnp.concatenate([keys, values], axis=1)
    low_halo, high_halo = exchange(pairs[:WIN], pairs[tokens - WIN:])
    low_seg, high_seg = exchange(segment_ids[:WIN], segment_ids[tokens - WIN:])
    low_seg = jnp.where(me == 0, -1, low_seg)
    high_seg = jnp.where(me == devices - 1, -1, high_seg)
    wide_seg = jnp.concatenate([low_seg, segment_ids, high_seg])
    queries = jnp.dot(activations, weight[:, :width], preferred_element_type=F32).astype(BF16)
    queries = (rope(queries).astype(BF16) * BF16(HD ** -0.5)).astype(BF16)
    head_grads = jnp.dot(out_grad, out_weight, preferred_element_type=F32).astype(BF16)
    attended, query_grad, key_grad, value_grad, rim_low, rim_high = attention(
        queries, head_grads, low_halo, pairs, high_halo, segment_ids[None, :], wide_seg[:, None], cos_t, sin_t
    )
    from_low, from_high = exchange(rim_low, rim_high)
    query_part = lax.dot_general(activations, query_grad, (((0,), (0,)), ((), ())),
                                 preferred_element_type=F32).astype(BF16)
    out_part = lax.dot_general(out_grad, attended, (((0,), (0,)), ((), ())), preferred_element_type=F32)
    arrived = jnp.concatenate(
        [from_low, jnp.zeros((tokens - 2 * WIN, 2 * width), BF16), from_high], axis=0
    ).astype(F32)
    key_grad = key_grad[WIN:WIN + tokens] + arrived[:, :width]
    value_grad = value_grad[WIN:WIN + tokens] + arrived[:, width:]
    low, high = key_grad[:, :half], key_grad[:, half:]
    qkv_grad = jnp.concatenate(
        [query_grad, (low * cos + high * sin).astype(BF16), (high * cos - low * sin).astype(BF16),
         value_grad.astype(BF16)], axis=1
    )
    rest_part = lax.dot_general(activations, qkv_grad[:, width:], (((0,), (0,)), ((), ())),
                                preferred_element_type=F32).astype(BF16)
    qkv_part = lax.dot_general(jnp.concatenate([query_part, rest_part], axis=1), order, NT,
                               preferred_element_type=F32)
    sums = jnp.concatenate([qkv_part.astype(BF16), out_part.astype(BF16)], axis=1)
    return reduce_all(qkv_grad, weight, sums)


def solution(mesh):
    in_specs = (
        P(("groups", "ctx"), None),
        P(("groups", "ctx"), None),
        P(("groups", "ctx")),
        P(None, "head"),
        P(None, "head"),
    )
    out_specs = (
        P(("groups", "ctx"), "head"),
        P(("groups", "ctx"), "head"),
        P(("groups", "ctx"), "head"),
    )
    return jax.shard_map(local, mesh=mesh, in_specs=in_specs, out_specs=out_specs, check_vma=False)
```
